32 devices in a mesh: box: 8 (over z, y), op: 4 (over x, core).
Axes of the slice: x: 2, y: 2, z: 4, core: 2. Of those that a mesh axis runs over, the one named last changes fastest.
Arguments:
- density: float32 [2304, 296], P(('box', 'op')), may hold values from -6 to 6
- operators: float32 [64, 296, 296], P('op'), may hold values from -0.046875 to 0.046875
- owner_count: int32 [8], replicated, may hold values from 96 to 288, as said below
- group_count: int32 [8], replicated, may hold values from 96 to 288, as said below
- target_slot: int32 [8, 64, 288], P('box', 'op'), may hold values from 0 to 288, as said below
- source_box: int32 [8, 64, 288], P('box', 'op'), may hold values from 0 to 1535, as said below
Outputs:
- check_potential: float32 [2304, 296], P(('box', 'op'))
The draws below stay inside these ranges and needn't reach their ends.
Inputs may be any that keep to these rules, and one draw needn't show every extreme that they name: `owner_count`: the counts sum to 1536. The start of owner d and the start of group d (sums of earlier counts) lie within 48 of d * 192, so they differ by at most 96, and some owner holds exactly 288 boxes. `group_count`: the counts sum to 1536, starts as for owner_count; some group holds exactly 288 boxes, and in every draw some group start lies 96 above the owner start of the same index. `target_slot`: entry j of a list of group g holds j or 288; where it holds j, j is below group_count[g]. `source_box`: an entry of group g's lists lies between group_start[g] - 96 and group_start[g + 1] + 96 - 1 (group_start[8] = 1536).
All inputs are finite; a program needn't handle non-finite values.
Results may differ from the reference program's by a relative error of at most 0.0001.
Values sent between devices are 32-bit elements; how exact they have to be, the bound alone decides.
No kernel may reach another device: no remote copies, remote signals or barrier semaphores. Data moves between devices by JAX's collectives and lax.ppermute only.
A program may use at most 64 MiB of HBM per device.

```python
import jax
import jax.numpy as jnp
from jax import lax

P_SIZE = 296
BD = 192
OFFSETS = 64
GROUPS = 8
BOXES = 1536
CAP = 288
HALF = 96
SLOTS = 2304


def layout_counts(key):
    base_key = jax.random.fold_in(key, 7)
    key_owner, key_group, key_rank = jax.random.split(base_key, 3)
    quarter = BD // 4
    forced_rank = jax.random.randint(key_rank, (), 2, GROUPS - 2)
    owner_off = jax.random.randint(key_owner, (GROUPS + 1,), -quarter, quarter + 1)
    group_off = jax.random.randint(key_group, (GROUPS + 1,), -quarter, quarter + 1)
    owner_off = owner_off.at[forced_rank].set(-quarter).at[forced_rank + 1].set(quarter).at[forced_rank + 2].set(-quarter)
    group_off = group_off.at[forced_rank - 1].set(-quarter).at[forced_rank].set(quarter).at[forced_rank + 1].set(-quarter)
    owner_off = owner_off.at[0].set(0).at[GROUPS].set(0)
    group_off = group_off.at[0].set(0).at[GROUPS].set(0)
    owner_count = (BD + owner_off[1:] - owner_off[:-1]).astype(jnp.int32)
    group_count = (BD + group_off[1:] - group_off[:-1]).astype(jnp.int32)
    return (owner_count, group_count)


def list_entries(key):
    group_count = layout_counts(key)[1]
    group_start = jnp.cumsum(group_count, dtype=jnp.int32) - group_count
    list_key = jax.random.fold_in(key, 11)
    key_keep, key_move = jax.random.split(list_key, 2)
    shape = (GROUPS, OFFSETS, CAP)
    entry_ids = jnp.arange(CAP, dtype=jnp.int32)[None, None, :]
    offset_ids = jnp.arange(OFFSETS, dtype=jnp.int32)[None, :, None]
    gcount = group_count[:, None, None]
    first_list = offset_ids == 0
    at_start = first_list & (entry_ids == 0)
    at_end = first_list & (entry_ids == gcount - 1)
    keep_entry = jax.random.randint(key_keep, shape, 0, 10) < 7
    keep_entry = keep_entry | at_start | at_end
    live_mask = keep_entry & (entry_ids < gcount)
    target_slot = jnp.where(live_mask, entry_ids, CAP).astype(jnp.int32)
    displace = jax.random.randint(key_move, shape, -HALF, HALF + 1)
    displace = jnp.where(at_start, -HALF, displace)
    displace = jnp.where(at_end, HALF, displace)
    base_box = group_start[:, None, None] + jnp.minimum(entry_ids, gcount - 1)
    source_box = jnp.clip(base_box + displace, 0, BOXES - 1).astype(jnp.int32)
    return (target_slot, source_box)


def draw_owner_count(key, part):
    return layout_counts(key)[0]


def draw_group_count(key, part):
    return layout_counts(key)[1]


def draw_target_slot(key, part):
    return list_entries(key)[0]


def draw_source_box(key, part):
    return list_entries(key)[1]


def steps_of(stream_key, dims, cuts, low, largest):
    loudness = 1.0
    for position, shards_of in cuts:
        heights = jax.random.uniform(jax.random.fold_in(jax.random.fold_in(stream_key, 6), position), (shards_of,), jnp.float32, low / len(cuts), largest / len(cuts))
        loudness = loudness * jnp.repeat(jnp.exp(heights), dims[position] // shards_of).reshape((-1,) + (1,) * (len(dims) - 1 - position))
    return loudness


def noise(own_key, shape, width, most, shards=(), kind=jnp.bfloat16):
    level = steps_of(own_key, shape, shards, -0.22, 0.18) if shards else 1.0
    result = jax.random.normal(own_key, shape, jnp.float32) * width * level
    return jnp.minimum(jnp.maximum(result, -most), most).astype(kind)


def setup_inputs(seed: int = 0) -> dict:
    key_list = jax.random.split(jax.random.key(seed), 7)
    return {
        "density": noise(key_list[0], (SLOTS, P_SIZE), 1.0, 6.0, ((0, 32),), jnp.float32),
        "operators": noise(key_list[1], (OFFSETS, P_SIZE, P_SIZE), (P_SIZE * OFFSETS) ** -0.5, 0.046875, ((0, 4),), jnp.float32),
        "owner_count": draw_owner_count(jax.random.fold_in(key_list[6], 71), 0),
        "group_count": draw_group_count(jax.random.fold_in(key_list[6], 71), 0),
        "target_slot": draw_target_slot(jax.random.fold_in(key_list[6], 71), 0),
        "source_box": draw_source_box(jax.random.fold_in(key_list[6], 71), 0),
    }


def exclusive_starts(counts):
    return jnp.cumsum(counts, dtype=jnp.int32) - counts


def reference(density, operators, owner_count, group_count, target_slot, source_box):
    owner_start = exclusive_starts(owner_count)
    group_start = exclusive_starts(group_count)
    slot_ids = jnp.arange(SLOTS, dtype=jnp.int32)
    owner_ids = slot_ids // CAP
    inner_ids = slot_ids % CAP
    occupied = inner_ids < owner_count[owner_ids]
    morton = jnp.where(occupied, owner_start[owner_ids] + inner_ids, BOXES).astype(jnp.int32)
    box_density = jnp.zeros((BOXES + 1, P_SIZE), jnp.float32).at[morton].set(density)[:BOXES]
    target_box = jnp.where(target_slot < CAP, group_start[:, None, None] + target_slot, BOXES).astype(jnp.int32)

    def offset_step(potential, offset_id):
        source_ids = source_box[:, offset_id, :].reshape(-1)
        target_ids = target_box[:, offset_id, :].reshape(-1)
        source_rows = box_density[source_ids]
        contrib = jnp.dot(source_rows, operators[offset_id].T, precision=lax.Precision.HIGHEST)
        return potential.at[target_ids].add(contrib), None

    potential, _ = lax.scan(offset_step, jnp.zeros((BOXES + 1, P_SIZE), jnp.float32), jnp.arange(OFFSETS, dtype=jnp.int32))
    return jnp.where(occupied[:, None], potential[morton], 0.0)
```

```python
import functools

import jax
import jax.numpy as jnp
from jax import lax
from jax.experimental import pallas as pl
from jax.experimental.pallas import tpu as pltpu
from jax.sharding import PartitionSpec as P

LANES = 128


def padded(size, to=LANES):
    return -(-size // to) * to


def shifted(pairs_axis, step):
    count = lax.axis_size(pairs_axis)
    return [(i, i + step) for i in range(count) if 0 <= i + step < count]


def flip(block, bit):
    count = lax.axis_size("op")
    return lax.ppermute(block, "op", [(i, i ^ bit) for i in range(count)])


def to_box(block, step):
    return lax.ppermute(block, "box", shifted("box", step))


def prefix(count_ref, upto):
    return lax.fori_loop(0, upto, lambda i, total: total + count_ref[i], 0)


def places(owner_ref, group_ref, box, boxes, capacity):
    before = jnp.maximum(box - 1, 0)
    after = jnp.minimum(box + 1, boxes - 1)
    own_start = prefix(owner_ref, box)
    own_count = owner_ref[box]
    prev_count = jnp.where(box > 0, owner_ref[before], 0)
    prev_start = own_start - jnp.where(box > 0, prev_count, capacity)
    next_start = own_start + own_count
    next_count = jnp.where(box < boxes - 1, owner_ref[after], 0)
    return (
        (prev_start, own_start, next_start),
        (prev_count, own_count, next_count),
        prefix(group_ref, box),
    )


def operator_kernel(op_ref, out_ref, *, size, whole):
    tail = size - whole
    block = op_ref[0]
    high = block.astype(jnp.bfloat16)
    low = block - high.astype(jnp.float32)
    out_ref[0, :, :whole] = high[:, :whole]
    out_ref[0, :, whole : 2 * whole] = low[:, :whole].astype(jnp.bfloat16)
    room = jnp.zeros((size, LANES - tail), jnp.float32)
    high_tail = jnp.concatenate([high[:, whole:].astype(jnp.float32), room], axis=1)
    low_tail = jnp.concatenate([low[:, whole:], room], axis=1)
    rest = high_tail + pltpu.roll(high_tail, tail, 1) + pltpu.roll(low_tail, 2 * tail, 1)
    out_ref[0, :, 2 * whole :] = rest.astype(jnp.bfloat16)


def split_operators(operators):
    count, size, _ = operators.shape
    whole = size // LANES * LANES
    width = 2 * whole + LANES
    return pl.pallas_call(
        functools.partial(operator_kernel, size=size, whole=whole),
        grid=(count,),
        in_specs=[pl.BlockSpec((1, size, size), lambda k: (k, 0, 0))],
        out_specs=pl.BlockSpec((1, size, width), lambda k: (k, 0, 0)),
        out_shape=jax.ShapeDtypeStruct((count, size, width), jnp.bfloat16),
        cost_estimate=pl.CostEstimate(
            flops=0, transcendentals=0, bytes_accessed=count * size * (4 * size + 2 * width)
        ),
        name="split_operators",
    )(operators)


def select_kernel(owner_ref, group_ref, target_ref, source_ref, out_ref, side_ref, *, boxes, capacity, quarter, span):
    box = lax.axis_index("box")
    core = lax.axis_index("op") % 2
    starts, _, group_start = places(owner_ref, group_ref, box, boxes, capacity)
    first = group_start - capacity // 3
    alive = target_ref[0] < capacity
    found = jnp.where(alive, source_ref[0] - first, -1)
    offsets = found.shape[0]
    found = jnp.concatenate(
        [found, jnp.full((offsets, padded(capacity) - capacity), -1, jnp.int32)], axis=1
    )
    columns = found.T
    row = lax.broadcasted_iota(jnp.int32, (capacity, span), 1)
    for k in range(offsets):
        hit = columns[:capacity, k : k + 1] == row
        out_ref[k] = jnp.where(hit, 1.0, 0.0).astype(jnp.bfloat16)
    tail = group_start + group_ref[box] - starts[1]
    slot = quarter * core + lax.broadcasted_iota(jnp.int32, side_ref.shape, 0)
    side_ref[...] = jnp.where(slot >= tail, 1.0, 0.0)


def selections(owner_count, group_count, target_slot, source_box, boxes, quarter, span):
    _, offsets, capacity = target_slot.shape
    smem = pl.BlockSpec(memory_space=pltpu.SMEM)
    vmem = pl.BlockSpec(memory_space=pltpu.VMEM)
    return pl.pallas_call(
        functools.partial(
            select_kernel, boxes=boxes, capacity=capacity, quarter=quarter, span=span
        ),
        in_specs=[smem, smem, vmem, vmem],
        out_specs=[vmem, vmem],
        out_shape=[
            jax.ShapeDtypeStruct((offsets, capacity, span), jnp.bfloat16),
            jax.ShapeDtypeStruct((quarter, LANES), jnp.float32),
        ],
        cost_estimate=pl.CostEstimate(
            flops=0, transcendentals=0, bytes_accessed=2 * offsets * capacity * span
        ),
        name="selections",
    )(owner_count, group_count, target_slot, source_box)


def translate_kernel(
    owner_ref,
    group_ref,
    own_ref,
    own_peer_ref,
    near_ref,
    near_peer_ref,
    weight_ref,
    pick_ref,
    send_ref,
    keep_ref,
    window,
    packed,
    total,
    *,
    boxes,
    capacity,
    quarter,
    size,
    span,
    need,
):
    step = pl.program_id(0)
    box = lax.axis_index("box")
    device = lax.axis_index("op")
    core = device % 2
    whole = size // LANES * LANES
    tail = size - whole
    third = capacity // 3
    tiles = padded(size) // LANES
    starts, counts, group_start = places(owner_ref, group_ref, box, boxes, capacity)

    def columns(tile):
        return slice(tile * LANES, min((tile + 1) * LANES, size))

    @pl.when(step == 0)
    def _():
        margin = 2 * third
        for tile in range(tiles):
            window[tile, margin + need : margin + span, :] = jnp.zeros((span - need, LANES), jnp.float32)
        for owner in range(3):
            for part in range(4):
                at = margin + starts[owner] + quarter * part - (group_start - third)
                at = jnp.clip(at, 0, window.shape[1] - quarter)
                mask = device ^ part
                line = pl.multiple_of(
                    jnp.where(mask >= 2, quarter * (1 if owner == 1 else 2), 0)
                    + (quarter if owner == 2 else 0),
                    8,
                )
                mine, peers = (own_ref, own_peer_ref) if owner == 1 else (near_ref, near_peer_ref)

                def put(source):
                    for tile in range(tiles):
                        lanes = columns(tile)
                        window[tile, pl.ds(at, quarter), : lanes.stop - lanes.start] = source[
                            pl.ds(line, quarter), lanes
                        ]

                pl.when(mask % 2 == 0)(functools.partial(put, mine))
                pl.when(mask % 2 == 1)(functools.partial(put, peers))
        for tile in range(tiles):
            value = window[tile, margin : margin + span, :]
            row = lax.broadcasted_iota(jnp.int32, value.shape, 0)
            lane = lax.broadcasted_iota(jnp.int32, value.shape, 1)
            fine = row < need
            if tile == tiles - 1:
                fine = fine & (lane < tail)
            value = jnp.where(fine, value, 0.0)
            high = value.astype(jnp.bfloat16)
            low = value - high.astype(jnp.float32)
            if tile < tiles - 1:
                packed[:, tile * LANES : (tile + 1) * LANES] = high
                packed[:, whole + tile * LANES : whole + (tile + 1) * LANES] = low.astype(jnp.bfloat16)
            else:
                high = high.astype(jnp.float32)
                rest = high + pltpu.roll(low, tail, 1) + pltpu.roll(high, 2 * tail, 1)
                packed[:, 2 * whole :] = rest.astype(jnp.bfloat16)
        total[...] = jnp.zeros(total.shape, jnp.float32)

    picked = jnp.dot(pick_ref[0], packed[...], preferred_element_type=jnp.float32).astype(jnp.bfloat16)
    weight = weight_ref[0]
    left = jnp.concatenate([picked[:, : 2 * whole], picked[:, :whole], picked[:, 2 * whole :]], axis=1)
    right = jnp.concatenate([weight[:, :whole], weight], axis=1)
    part = lax.dot_general(left, right, (((1,), (1,)), ((), ())), preferred_element_type=jnp.float32)
    for tile in range(tiles):
        lanes = columns(tile)
        total[tile, capacity : 2 * capacity, : lanes.stop - lanes.start] += part[:, lanes]

    @pl.when(step == pl.num_programs(0) - 1)
    def _():
        def rows(owner, block):
            at = capacity + starts[owner] - group_start + quarter * block
            at = jnp.clip(at, 0, total.shape[1] - quarter)
            slot = quarter * block + lax.broadcasted_iota(jnp.int32, (quarter, 1), 0)
            value = jnp.concatenate([total[tile, pl.ds(at, quarter), :] for tile in range(tiles)], axis=1)
            return jnp.where(slot < counts[owner], value, 0.0)[:, :size]

        for ref, side in ((keep_ref, core), (send_ref, 1 - core)):
            ref[:quarter] = rows(1, side)
            ref[quarter : 2 * quarter] = rows(1, side + 2)
            ref[2 * quarter : 3 * quarter] = rows(0, side) + rows(0, side + 2)
            ref[3 * quarter :] = rows(2, side)


def translate(owner_count, group_count, own, own_peer, near, near_peer, weights, picks, boxes):
    offsets, capacity, span = picks.shape
    size = weights.shape[1]
    width = weights.shape[2]
    quarter = own.shape[0] // 2
    need = capacity + 2 * (capacity // 3)
    tiles = padded(size) // LANES
    smem = pl.BlockSpec(memory_space=pltpu.SMEM)
    vmem = pl.BlockSpec(memory_space=pltpu.VMEM)
    return pl.pallas_call(
        functools.partial(
            translate_kernel,
            boxes=boxes,
            capacity=capacity,
            quarter=quarter,
            size=size,
            span=span,
            need=need,
        ),
        grid=(offsets,),
        in_specs=[
            smem,
            smem,
            vmem,
            vmem,
            vmem,
            vmem,
            pl.BlockSpec((1, size, width), lambda k: (k, 0, 0)),
            pl.BlockSpec((1, capacity, span), lambda k: (k, 0, 0)),
        ],
        out_specs=[vmem, vmem],
        out_shape=[jax.ShapeDtypeStruct((capacity, size), jnp.float32)] * 2,
        scratch_shapes=[
            pltpu.VMEM((tiles, 3 * capacity, LANES), jnp.float32),
            pltpu.VMEM((span, width), jnp.bfloat16),
            pltpu.VMEM((tiles, 3 * capacity, LANES), jnp.float32),
        ],
        name="translate",
    )(owner_count, group_count, own, own_peer, near, near_peer, weights, picks)


def body(density, operators, owner_count, group_count, target_slot, source_box):
    quarter = density.shape[0]
    parts = lax.axis_size("op")
    boxes = lax.axis_size("box")
    capacity = quarter * parts
    if parts != 4:
        raise ValueError("unsupported op axis")
    span = padded(capacity + 2 * (capacity // 3))
    device = lax.axis_index("op")

    earlier = to_box(density, 1)
    later = to_box(density, -1)
    across = flip(density, 2)
    weights = split_operators(operators)
    picks, side = selections(
        owner_count, group_count, target_slot, source_box, boxes, quarter, span
    )
    own = jnp.concatenate([density, across], axis=0)
    own_peer = flip(own, 1)
    near = jnp.concatenate([earlier, later], axis=0)
    near = jnp.concatenate([near, flip(near, 2)], axis=0)
    near_peer = flip(near, 1)
    send, keep = translate(
        owner_count, group_count, own, own_peer, near, near_peer, weights, picks, boxes
    )
    both = keep + flip(send, 1)
    low, high, down, up = (both[i * quarter : (i + 1) * quarter] for i in range(4))
    from_after = to_box(down, -1)
    from_before = to_box(up, 1)
    early = side[:, :1] > 0.5
    low = low + from_before + jnp.where(early, from_after, 0.0)
    high = high + jnp.where(early, 0.0, from_after)
    first = device < 2
    return jnp.where(first, low, high) + flip(jnp.where(first, high, low), 2)


def solution(mesh):
    placed = (
        P(("box", "op"), None),
        P("op", None, None),
        P(),
        P(),
        P("box", "op", None),
        P("box", "op", None),
    )
    return jax.shard_map(
        body, mesh=mesh, in_specs=placed, out_specs=P(("box", "op"), None), check_vma=False
    )
```

```python
import functools
import math

import jax
import jax.numpy as jnp
from jax import lax
from jax.experimental import pallas as pl
from jax.experimental.pallas import tpu as pltpu
from jax.sharding import PartitionSpec as P

LANES = 128
GRANT = 20 << 20
BATCH = 2


def padded(size, to=LANES):
    return -(-size // to) * to


def shifted(pairs_axis, step):
    count = lax.axis_size(pairs_axis)
    return [(i, i + step) for i in range(count) if 0 <= i + step < count]


def flip(block, bit):
    count = lax.axis_size("op")
    return lax.ppermute(block, "op", [(i, i ^ bit) for i in range(count)])


def to_box(block, step):
    return lax.ppermute(block, "box", shifted("box", step))


def prefix(count_ref, upto):
    return lax.fori_loop(0, upto, lambda i, total: total + count_ref[i], 0)


def places(owner_ref, group_ref, box, boxes, capacity):
    before = jnp.maximum(box - 1, 0)
    after = jnp.minimum(box + 1, boxes - 1)
    own_start = prefix(owner_ref, box)
    own_count = owner_ref[box]
    prev_count = jnp.where(box > 0, owner_ref[before], 0)
    prev_start = own_start - jnp.where(box > 0, prev_count, capacity)
    next_start = own_start + own_count
    next_count = jnp.where(box < boxes - 1, owner_ref[after], 0)
    return (
        (prev_start, own_start, next_start),
        (prev_count, own_count, next_count),
        prefix(group_ref, box),
    )


def operator_kernel(op_ref, main_ref, rest_ref, *, size, whole, room):
    tail = size - whole

    def split(k, carry):
        block = op_ref[k]
        high = block.astype(jnp.bfloat16)
        wide = high.astype(jnp.float32)
        low = block - wide
        space = jnp.zeros((size, LANES - tail), jnp.float32)
        high_tail = jnp.concatenate([wide[:, whole:], space], axis=1)
        low_tail = jnp.concatenate([low[:, whole:], space], axis=1)
        ends = high_tail + pltpu.roll(high_tail, tail, 1) + pltpu.roll(low_tail, 2 * tail, 1)
        low = low[:, :whole].astype(jnp.bfloat16)
        ends = ends.astype(jnp.bfloat16)
        main_ref[k, :, :whole] = high[:whole, :whole]
        main_ref[k, :, whole : 2 * whole] = low[:whole]
        main_ref[k, :, 2 * whole :] = ends[:whole]
        blank = jnp.zeros((room - tail, whole), jnp.bfloat16)
        first = jnp.concatenate([high[whole:, :whole], blank], axis=0)
        rest_ref[k, :room, :whole] = first
        rest_ref[k, :room, whole : 2 * whole] = first
        rest_ref[k, :room, 2 * whole :] = jnp.concatenate([ends[whole:], blank[:, :LANES]], axis=0)
        rest_ref[k, room:, :whole] = jnp.concatenate([low[whole:], blank], axis=0)
        rest_ref[k, room:, whole:] = jnp.zeros((room, whole + LANES), jnp.bfloat16)
        return carry

    lax.fori_loop(0, op_ref.shape[0], split, 0)


def split_operators(operators):
    count, size, _ = operators.shape
    whole = size // LANES * LANES
    room = padded(size - whole, 16)
    width = 2 * whole + LANES
    vmem = pl.BlockSpec(memory_space=pltpu.VMEM)
    return pl.pallas_call(
        functools.partial(operator_kernel, size=size, whole=whole, room=room),
        in_specs=[vmem],
        out_specs=[vmem, vmem],
        out_shape=[
            jax.ShapeDtypeStruct((count, whole, width), jnp.bfloat16),
            jax.ShapeDtypeStruct((count, 2 * room, width), jnp.bfloat16),
        ],
        compiler_params=pltpu.CompilerParams(vmem_limit_bytes=GRANT),
        cost_estimate=pl.CostEstimate(
            flops=0, transcendentals=0, bytes_accessed=count * size * (4 * size + 2 * width)
        ),
        name="split_operators",
    )(operators)


def select_kernel(owner_ref, group_ref, target_ref, source_ref, out_ref, side_ref, *, boxes, capacity, quarter, span):
    box = lax.axis_index("box")
    core = lax.axis_index("op") % 2
    starts, _, group_start = places(owner_ref, group_ref, box, boxes, capacity)
    first = group_start - capacity // 3
    alive = target_ref[0] < capacity
    found = jnp.where(alive, source_ref[0] - first, -1)
    offsets = found.shape[0]
    found = jnp.concatenate(
        [found, jnp.full((offsets, padded(capacity) - capacity), -1, jnp.int32)], axis=1
    )
    columns = found.T
    row = lax.broadcasted_iota(jnp.int32, (capacity, span), 1)
    for k in range(offsets):
        hit = columns[:capacity, k : k + 1] == row
        out_ref[k] = jnp.where(hit, 1.0, 0.0).astype(jnp.bfloat16)
    tail = group_start + group_ref[box] - starts[1]
    slot = quarter * core + lax.broadcasted_iota(jnp.int32, side_ref.shape, 0)
    side_ref[...] = jnp.where(slot >= tail, 1.0, 0.0)


def selections(owner_count, group_count, target_slot, source_box, boxes, quarter, span):
    _, offsets, capacity = target_slot.shape
    smem = pl.BlockSpec(memory_space=pltpu.SMEM)
    vmem = pl.BlockSpec(memory_space=pltpu.VMEM)
    return pl.pallas_call(
        functools.partial(
            select_kernel, boxes=boxes, capacity=capacity, quarter=quarter, span=span
        ),
        in_specs=[smem, smem, vmem, vmem],
        out_specs=[vmem, vmem],
        out_shape=[
            jax.ShapeDtypeStruct((offsets, capacity, span), jnp.bfloat16),
            jax.ShapeDtypeStruct((quarter, LANES), jnp.float32),
        ],
        compiler_params=pltpu.CompilerParams(vmem_limit_bytes=GRANT),
        cost_estimate=pl.CostEstimate(
            flops=0, transcendentals=0, bytes_accessed=2 * offsets * capacity * span
        ),
        name="selections",
    )(owner_count, group_count, target_slot, source_box)


def translate_kernel(
    owner_ref,
    group_ref,
    own_ref,
    own_peer_ref,
    near_ref,
    near_peer_ref,
    weight_ref,
    rest_ref,
    pick_ref,
    send_ref,
    keep_ref,
    window,
    packed,
    total,
    ends,
    *,
    boxes,
    capacity,
    quarter,
    size,
    span,
    need,
    batch,
):
    box = lax.axis_index("box")
    device = lax.axis_index("op")
    core = device % 2
    whole = size // LANES * LANES
    tail = size - whole
    third = capacity // 3
    tiles = padded(size) // LANES
    room = rest_ref.shape[1] // 2
    starts, counts, group_start = places(owner_ref, group_ref, box, boxes, capacity)

    def columns(tile):
        return slice(tile * LANES, min((tile + 1) * LANES, size))

    margin = 2 * third
    for tile in range(tiles):
        window[tile, margin + need : margin + span, :] = jnp.zeros((span - need, LANES), jnp.float32)
    for owner in range(3):
        for part in range(4):
            at = margin + starts[owner] + quarter * part - (group_start - third)
            at = jnp.clip(at, 0, window.shape[1] - quarter)
            mask = device ^ part
            line = pl.multiple_of(
                jnp.where(mask >= 2, quarter * (1 if owner == 1 else 2), 0)
                + (quarter if owner == 2 else 0),
                8,
            )
            mine, peers = (own_ref, own_peer_ref) if owner == 1 else (near_ref, near_peer_ref)

            def put(source):
                for tile in range(tiles):
                    lanes = columns(tile)
                    window[tile, pl.ds(at, quarter), : lanes.stop - lanes.start] = source[
                        pl.ds(line, quarter), lanes
                    ]

            pl.when(mask % 2 == 0)(functools.partial(put, mine))
            pl.when(mask % 2 == 1)(functools.partial(put, peers))
    for tile in range(tiles):
        value = window[tile, margin : margin + span, :]
        row = lax.broadcasted_iota(jnp.int32, value.shape, 0)
        lane = lax.broadcasted_iota(jnp.int32, value.shape, 1)
        fine = row < need
        if tile == tiles - 1:
            fine = fine & (lane < tail)
        value = jnp.where(fine, value, 0.0)
        high = value.astype(jnp.bfloat16)
        low = value - high.astype(jnp.float32)
        if tile < tiles - 1:
            packed[:, tile * LANES : (tile + 1) * LANES] = high
            packed[:, whole + tile * LANES : whole + (tile + 1) * LANES] = low.astype(jnp.bfloat16)
        else:
            high = high.astype(jnp.float32)
            rest = high + pltpu.roll(low, tail, 1) + pltpu.roll(high, 2 * tail, 1)
            packed[:, 2 * whole :] = rest.astype(jnp.bfloat16)
    total[...] = jnp.zeros(total.shape, jnp.float32)
    ends[...] = jnp.zeros(ends.shape, jnp.float32)

    def product(left, right):
        return lax.dot_general(
            jnp.concatenate(left, axis=1),
            jnp.concatenate(right, axis=1),
            (((1,), (1,)), ((), ())),
            preferred_element_type=jnp.float32,
        )

    def offsets(index, carry):
        base = index * batch
        picks = pick_ref[pl.ds(base, batch)].reshape(batch * capacity, span)
        picked = jnp.dot(picks, packed[...], preferred_element_type=jnp.float32).astype(jnp.bfloat16)
        left, right, left_ends, right_ends = [], [], [], []
        for i in range(batch):
            rows = picked[i * capacity : (i + 1) * capacity]
            weight = weight_ref[base + i]
            left += [rows[:, : 2 * whole], rows[:, :whole]]
            right += [weight[:, :whole], weight[:, : 2 * whole]]
            left_ends += [rows[:, : 2 * whole]]
            right_ends += [rest_ref[base + i, :, : 2 * whole]]
        for i in range(batch):
            last = picked[i * capacity : (i + 1) * capacity, 2 * whole :]
            left += [last]
            right += [weight_ref[base + i, :, 2 * whole :]]
            left_ends += [last]
            right_ends += [rest_ref[base + i, :, 2 * whole :]]
        part = product(left, right)
        for tile in range(tiles - 1):
            total[tile, capacity : 2 * capacity, :] += part[:, tile * LANES : (tile + 1) * LANES]
        ends[:, : 2 * room] += product(left_ends, right_ends)
        return carry

    lax.fori_loop(0, pick_ref.shape[0] // batch, offsets, 0)
    both = ends[...]
    total[tiles - 1, capacity : 2 * capacity, :] = both + pltpu.roll(both, LANES - room, 1)

    def rows(owner, block):
        at = capacity + starts[owner] - group_start + quarter * block
        at = jnp.clip(at, 0, total.shape[1] - quarter)
        slot = quarter * block + lax.broadcasted_iota(jnp.int32, (quarter, 1), 0)
        value = jnp.concatenate([total[tile, pl.ds(at, quarter), :] for tile in range(tiles)], axis=1)
        return jnp.where(slot < counts[owner], value, 0.0)[:, :size]

    for ref, side in ((keep_ref, core), (send_ref, 1 - core)):
        ref[:quarter] = rows(1, side)
        ref[quarter : 2 * quarter] = rows(1, side + 2)
        ref[2 * quarter : 3 * quarter] = rows(0, side) + rows(0, side + 2)
        ref[3 * quarter :] = rows(2, side)


def translate(owner_count, group_count, own, own_peer, near, near_peer, weights, rests, picks, boxes):
    offsets, capacity, span = picks.shape
    width = weights.shape[2]
    size = own.shape[1]
    quarter = own.shape[0] // 2
    need = capacity + 2 * (capacity // 3)
    tiles = padded(size) // LANES
    smem = pl.BlockSpec(memory_space=pltpu.SMEM)
    vmem = pl.BlockSpec(memory_space=pltpu.VMEM)
    return pl.pallas_call(
        functools.partial(
            translate_kernel,
            boxes=boxes,
            capacity=capacity,
            quarter=quarter,
            size=size,
            span=span,
            need=need,
            batch=math.gcd(offsets, BATCH),
        ),
        in_specs=[smem, smem] + [vmem] * 7,
        out_specs=[vmem, vmem],
        out_shape=[jax.ShapeDtypeStruct((capacity, size), jnp.float32)] * 2,
        scratch_shapes=[
            pltpu.VMEM((tiles, 3 * capacity, LANES), jnp.float32),
            pltpu.VMEM((span, width), jnp.bfloat16),
            pltpu.VMEM((tiles, 3 * capacity, LANES), jnp.float32),
            pltpu.VMEM((capacity, LANES), jnp.float32),
        ],
        compiler_params=pltpu.CompilerParams(vmem_limit_bytes=GRANT),
        name="translate",
    )(owner_count, group_count, own, own_peer, near, near_peer, weights, rests, picks)


def body(density, operators, owner_count, group_count, target_slot, source_box):
    quarter = density.shape[0]
    parts = lax.axis_size("op")
    boxes = lax.axis_size("box")
    capacity = quarter * parts
    if parts != 4:
        raise ValueError("unsupported op axis")
    span = padded(capacity + 2 * (capacity // 3))
    device = lax.axis_index("op")

    earlier = to_box(density, 1)
    later = to_box(density, -1)
    across = flip(density, 2)
    picks, side = selections(
        owner_count, group_count, target_slot, source_box, boxes, quarter, span
    )
    near = jnp.concatenate([earlier, later], axis=0)
    near, picks = lax.optimization_barrier((near, picks))
    near_across = flip(near, 2)
    own = jnp.concatenate([density, across], axis=0)
    own_peer = flip(own, 1)
    weights, rests = split_operators(operators)
    near_across, weights, rests = lax.optimization_barrier((near_across, weights, rests))
    near = jnp.concatenate([near, near_across], axis=0)
    near_peer = flip(near, 1)
    send, keep = translate(
        owner_count, group_count, own, own_peer, near, near_peer, weights, rests, picks, boxes
    )
    both = keep + flip(send, 1)
    low, high, down, up = (both[i * quarter : (i + 1) * quarter] for i in range(4))
    from_after = to_box(down, -1)
    from_before = to_box(up, 1)
    early = side[:, :1] > 0.5
    low = low + from_before + jnp.where(early, from_after, 0.0)
    high = high + jnp.where(early, 0.0, from_after)
    first = device < 2
    return jnp.where(first, low, high) + flip(jnp.where(first, high, low), 2)


def solution(mesh):
    placed = (
        P(("box", "op"), None),
        P("op", None, None),
        P(),
        P(),
        P("box", "op", None),
        P("box", "op", None),
    )
    return jax.shard_map(
        body, mesh=mesh, in_specs=placed, out_specs=P(("box", "op"), None), check_vma=False
    )
```

```python
import functools
import math

import jax
import jax.numpy as jnp
from jax import lax
from jax.experimental import pallas as pl
from jax.experimental.pallas import tpu as pltpu
from jax.sharding import PartitionSpec as P

LANES = 128
GRANT = 20 << 20
BATCH = 4


def padded(size, to=LANES):
    return -(-size // to) * to


def shifted(pairs_axis, step):
    count = lax.axis_size(pairs_axis)
    return [(i, i + step) for i in range(count) if 0 <= i + step < count]


def flip(block, bit):
    count = lax.axis_size("op")
    return lax.ppermute(block, "op", [(i, i ^ bit) for i in range(count)])


def to_box(block, step):
    return lax.ppermute(block, "box", shifted("box", step))


def prefix(count_ref, upto):
    return lax.fori_loop(0, upto, lambda i, total: total + count_ref[i], 0)


def places(owner_ref, group_ref, box, boxes, capacity):
    before = jnp.maximum(box - 1, 0)
    after = jnp.minimum(box + 1, boxes - 1)
    own_start = prefix(owner_ref, box)
    own_count = owner_ref[box]
    prev_count = jnp.where(box > 0, owner_ref[before], 0)
    prev_start = own_start - jnp.where(box > 0, prev_count, capacity)
    next_start = own_start + own_count
    next_count = jnp.where(box < boxes - 1, owner_ref[after], 0)
    return (
        (prev_start, own_start, next_start),
        (prev_count, own_count, next_count),
        prefix(group_ref, box),
    )


def prepare_kernel(
    owner_hbm,
    group_hbm,
    target_hbm,
    source_hbm,
    op_hbm,
    pick_ref,
    side_ref,
    main_ref,
    rest_ref,
    owner_ref,
    group_ref,
    target_ref,
    source_ref,
    op_ref,
    list_sem,
    op_sem,
    *,
    boxes,
    capacity,
    quarter,
    span,
    whole,
    room,
):
    offsets, size, _ = op_ref.shape
    tail = size - whole
    lists = [
        pltpu.make_async_copy(source, target, list_sem.at[i])
        for i, (source, target) in enumerate(
            (
                (target_hbm, target_ref),
                (source_hbm, source_ref),
                (owner_hbm, owner_ref),
                (group_hbm, group_ref),
            )
        )
    ]

    def fetch(k):
        return pltpu.make_async_copy(op_hbm.at[k], op_ref.at[k], op_sem.at[k])

    for copy in lists:
        copy.start()
    for k in range(offsets):
        fetch(k).start()
    for copy in lists:
        copy.wait()

    box = lax.axis_index("box")
    core = lax.axis_index("op") % 2
    starts, _, group_start = places(owner_ref, group_ref, box, boxes, capacity)
    first = group_start - capacity // 3
    found = jnp.where(target_ref[0] < capacity, source_ref[0] - first, -1)
    found = jnp.concatenate(
        [found, jnp.full((offsets, padded(capacity) - capacity), -1, jnp.int32)], axis=1
    )
    columns = found.T
    row = lax.broadcasted_iota(jnp.int32, (capacity, span), 1)
    for k in range(offsets):
        hit = columns[:capacity, k : k + 1] == row
        pick_ref[k] = jnp.where(hit, 1.0, 0.0).astype(jnp.bfloat16)
    bound = group_start + group_ref[box] - starts[1]
    slot = quarter * core + lax.broadcasted_iota(jnp.int32, side_ref.shape, 0)
    side_ref[...] = jnp.where(slot >= bound, 1.0, 0.0)

    def split(k, carry):
        fetch(k).wait()
        block = op_ref[k]
        high = block.astype(jnp.bfloat16)
        wide = high.astype(jnp.float32)
        low = block - wide
        space = jnp.zeros((size, LANES - tail), jnp.float32)
        high_tail = jnp.concatenate([wide[:, whole:], space], axis=1)
        low_tail = jnp.concatenate([low[:, whole:], space], axis=1)
        ends = high_tail + pltpu.roll(high_tail, tail, 1) + pltpu.roll(low_tail, 2 * tail, 1)
        low = low[:, :whole].astype(jnp.bfloat16)
        ends = ends.astype(jnp.bfloat16)
        main_ref[k, :, :whole] = high[:whole, :whole]
        main_ref[k, :, whole : 2 * whole] = low[:whole]
        main_ref[k, :, 2 * whole :] = ends[:whole]
        blank = jnp.zeros((room - tail, whole), jnp.bfloat16)
        top = jnp.concatenate([high[whole:, :whole], blank], axis=0)
        rest_ref[k, :room, :whole] = top
        rest_ref[k, :room, whole : 2 * whole] = top
        rest_ref[k, :room, 2 * whole :] = jnp.concatenate([ends[whole:], blank[:, :LANES]], axis=0)
        rest_ref[k, room:, :whole] = jnp.concatenate([low[whole:], blank], axis=0)
        rest_ref[k, room:, whole:] = jnp.zeros((room, whole + LANES), jnp.bfloat16)
        return carry

    lax.fori_loop(0, offsets, split, 0)


def prepare(owner_count, group_count, target_slot, source_box, operators, boxes, quarter, span):
    _, offsets, capacity = target_slot.shape
    size = operators.shape[1]
    whole = size // LANES * LANES
    room = padded(size - whole, 16)
    width = 2 * whole + LANES
    hbm = pl.BlockSpec(memory_space=pltpu.HBM)
    vmem = pl.BlockSpec(memory_space=pltpu.VMEM)
    return pl.pallas_call(
        functools.partial(
            prepare_kernel,
            boxes=boxes,
            capacity=capacity,
            quarter=quarter,
            span=span,
            whole=whole,
            room=room,
        ),
        in_specs=[hbm] * 5,
        out_specs=[vmem] * 4,
        out_shape=[
            jax.ShapeDtypeStruct((offsets, capacity, span), jnp.bfloat16),
            jax.ShapeDtypeStruct((quarter, LANES), jnp.float32),
            jax.ShapeDtypeStruct((offsets, whole, width), jnp.bfloat16),
            jax.ShapeDtypeStruct((offsets, 2 * room, width), jnp.bfloat16),
        ],
        scratch_shapes=[
            pltpu.SMEM(owner_count.shape, jnp.int32),
            pltpu.SMEM(group_count.shape, jnp.int32),
            pltpu.VMEM(target_slot.shape, jnp.int32),
            pltpu.VMEM(source_box.shape, jnp.int32),
            pltpu.VMEM(operators.shape, jnp.float32),
            pltpu.SemaphoreType.DMA((4,)),
            pltpu.SemaphoreType.DMA((offsets,)),
        ],
        compiler_params=pltpu.CompilerParams(vmem_limit_bytes=GRANT),
        cost_estimate=pl.CostEstimate(
            flops=0, transcendentals=0, bytes_accessed=4 * offsets * size * size
        ),
        name="prepare",
    )(
        *(
            pltpu.with_memory_space_constraint(value, pltpu.HBM)
            for value in (owner_count, group_count, target_slot, source_box, operators)
        )
    )


def translate_kernel(
    owner_ref,
    group_ref,
    own_ref,
    own_peer_ref,
    near_ref,
    near_peer_ref,
    weight_ref,
    rest_ref,
    pick_ref,
    send_ref,
    keep_ref,
    window,
    packed,
    total,
    ends,
    *,
    boxes,
    capacity,
    quarter,
    size,
    span,
    need,
    batch,
):
    box = lax.axis_index("box")
    device = lax.axis_index("op")
    core = device % 2
    whole = size // LANES * LANES
    tail = size - whole
    third = capacity // 3
    tiles = padded(size) // LANES
    room = rest_ref.shape[1] // 2
    starts, counts, group_start = places(owner_ref, group_ref, box, boxes, capacity)

    def columns(tile):
        return slice(tile * LANES, min((tile + 1) * LANES, size))

    margin = 2 * third
    for tile in range(tiles):
        window[tile, margin + need : margin + span, :] = jnp.zeros((span - need, LANES), jnp.float32)
    for owner in range(3):
        for part in range(4):
            at = margin + starts[owner] + quarter * part - (group_start - third)
            at = jnp.clip(at, 0, window.shape[1] - quarter)
            mask = device ^ part
            line = pl.multiple_of(
                jnp.where(mask >= 2, quarter * (1 if owner == 1 else 2), 0)
                + (quarter if owner == 2 else 0),
                8,
            )
            mine, peers = (own_ref, own_peer_ref) if owner == 1 else (near_ref, near_peer_ref)

            def put(source):
                for tile in range(tiles):
                    lanes = columns(tile)
                    window[tile, pl.ds(at, quarter), : lanes.stop - lanes.start] = source[
                        pl.ds(line, quarter), lanes
                    ]

            pl.when(mask % 2 == 0)(functools.partial(put, mine))
            pl.when(mask % 2 == 1)(functools.partial(put, peers))
    for tile in range(tiles):
        value = window[tile, margin : margin + span, :]
        row = lax.broadcasted_iota(jnp.int32, value.shape, 0)
        lane = lax.broadcasted_iota(jnp.int32, value.shape, 1)
        fine = row < need
        if tile == tiles - 1:
            fine = fine & (lane < tail)
        value = jnp.where(fine, value, 0.0)
        high = value.astype(jnp.bfloat16)
        low = value - high.astype(jnp.float32)
        if tile < tiles - 1:
            packed[:, tile * LANES : (tile + 1) * LANES] = high
            packed[:, whole + tile * LANES : whole + (tile + 1) * LANES] = low.astype(jnp.bfloat16)
        else:
            high = high.astype(jnp.float32)
            rest = high + pltpu.roll(low, tail, 1) + pltpu.roll(high, 2 * tail, 1)
            packed[:, 2 * whole :] = rest.astype(jnp.bfloat16)
    total[...] = jnp.zeros(total.shape, jnp.float32)
    ends[...] = jnp.zeros(ends.shape, jnp.float32)

    def product(left, right):
        return lax.dot_general(
            jnp.concatenate(left, axis=1),
            jnp.concatenate(right, axis=1),
            (((1,), (1,)), ((), ())),
            preferred_element_type=jnp.float32,
        )

    def offsets(index, carry):
        base = index * batch
        picks = pick_ref[pl.ds(base, batch)].reshape(batch * capacity, span)
        picked = jnp.dot(picks, packed[...], preferred_element_type=jnp.float32).astype(jnp.bfloat16)
        left, right, left_ends, right_ends = [], [], [], []
        for i in range(batch):
            rows = picked[i * capacity : (i + 1) * capacity]
            weight = weight_ref[base + i]
            left += [rows[:, : 2 * whole], rows[:, :whole]]
            right += [weight[:, :whole], weight[:, : 2 * whole]]
            left_ends += [rows[:, : 2 * whole]]
            right_ends += [rest_ref[base + i, :, : 2 * whole]]
        for i in range(batch):
            last = picked[i * capacity : (i + 1) * capacity, 2 * whole :]
            left += [last]
            right += [weight_ref[base + i, :, 2 * whole :]]
            left_ends += [last]
            right_ends += [rest_ref[base + i, :, 2 * whole :]]
        part = product(left, right)
        for tile in range(tiles - 1):
            total[tile, capacity : 2 * capacity, :] += part[:, tile * LANES : (tile + 1) * LANES]
        ends[:, : 2 * room] += product(left_ends, right_ends)
        return carry

    lax.fori_loop(0, pick_ref.shape[0] // batch, offsets, 0)
    both = ends[...]
    total[tiles - 1, capacity : 2 * capacity, :] = both + pltpu.roll(both, LANES - room, 1)

    def rows(owner, block):
        at = capacity + starts[owner] - group_start + quarter * block
        at = jnp.clip(at, 0, total.shape[1] - quarter)
        slot = quarter * block + lax.broadcasted_iota(jnp.int32, (quarter, 1), 0)
        value = jnp.concatenate([total[tile, pl.ds(at, quarter), :] for tile in range(tiles)], axis=1)
        return jnp.where(slot < counts[owner], value, 0.0)[:, :size]

    for ref, side in ((keep_ref, core), (send_ref, 1 - core)):
        ref[:quarter] = rows(1, side)
        ref[quarter : 2 * quarter] = rows(1, side + 2)
        ref[2 * quarter : 3 * quarter] = rows(0, side) + rows(0, side + 2)
        ref[3 * quarter :] = rows(2, side)


def translate(owner_count, group_count, own, own_peer, near, near_peer, weights, rests, picks, boxes):
    offsets, capacity, span = picks.shape
    width = weights.shape[2]
    size = own.shape[1]
    quarter = own.shape[0] // 2
    need = capacity + 2 * (capacity // 3)
    tiles = padded(size) // LANES
    smem = pl.BlockSpec(memory_space=pltpu.SMEM)
    vmem = pl.BlockSpec(memory_space=pltpu.VMEM)
    return pl.pallas_call(
        functools.partial(
            translate_kernel,
            boxes=boxes,
            capacity=capacity,
            quarter=quarter,
            size=size,
            span=span,
            need=need,
            batch=math.gcd(offsets, BATCH),
        ),
        in_specs=[smem, smem] + [vmem] * 7,
        out_specs=[vmem, vmem],
        out_shape=[jax.ShapeDtypeStruct((capacity, size), jnp.float32)] * 2,
        scratch_shapes=[
            pltpu.VMEM((tiles, 3 * capacity, LANES), jnp.float32),
            pltpu.VMEM((span, width), jnp.bfloat16),
            pltpu.VMEM((tiles, 3 * capacity, LANES), jnp.float32),
            pltpu.VMEM((capacity, LANES), jnp.float32),
        ],
        compiler_params=pltpu.CompilerParams(vmem_limit_bytes=GRANT),
        name="translate",
    )(owner_count, group_count, own, own_peer, near, near_peer, weights, rests, picks)


def body(density, operators, owner_count, group_count, target_slot, source_box):
    quarter = density.shape[0]
    parts = lax.axis_size("op")
    boxes = lax.axis_size("box")
    capacity = quarter * parts
    if parts != 4:
        raise ValueError("unsupported op axis")
    span = padded(capacity + 2 * (capacity // 3))
    device = lax.axis_index("op")

    earlier = to_box(density, 1)
    later = to_box(density, -1)
    across = flip(density, 2)
    near = jnp.concatenate([earlier, later], axis=0)
    own = jnp.concatenate([density, across], axis=0)
    near, own = lax.optimization_barrier((near, own))
    near_across = flip(near, 2)
    own_peer = flip(own, 1)
    picks, side, weights, rests = prepare(
        owner_count, group_count, target_slot, source_box, operators, boxes, quarter, span
    )
    near_across, own_peer, picks, weights, rests = lax.optimization_barrier(
        (near_across, own_peer, picks, weights, rests)
    )
    near = jnp.concatenate([near, near_across], axis=0)
    near_peer = flip(near, 1)
    send, keep = translate(
        owner_count, group_count, own, own_peer, near, near_peer, weights, rests, picks, boxes
    )
    both = keep + flip(send, 1)
    low, high, down, up = (both[i * quarter : (i + 1) * quarter] for i in range(4))
    from_after = to_box(down, -1)
    from_before = to_box(up, 1)
    early = side[:, :1] > 0.5
    low = low + from_before + jnp.where(early, from_after, 0.0)
    high = high + jnp.where(early, 0.0, from_after)
    first = device < 2
    return jnp.where(first, low, high) + flip(jnp.where(first, high, low), 2)


def solution(mesh):
    placed = (
        P(("box", "op"), None),
        P("op", None, None),
        P(),
        P(),
        P("box", "op", None),
        P("box", "op", None),
    )
    return jax.shard_map(
        body, mesh=mesh, in_specs=placed, out_specs=P(("box", "op"), None), check_vma=False
    )
```

```python
import functools
import math

import jax
import jax.numpy as jnp
from jax import lax
from jax.experimental import pallas as pl
from jax.experimental.pallas import tpu as pltpu
from jax.sharding import PartitionSpec as P

LANES = 128
GRANT = 20 << 20
BATCH = 2


def padded(size, to=LANES):
    return -(-size // to) * to


def shifted(pairs_axis, step):
    count = lax.axis_size(pairs_axis)
    return [(i, i + step) for i in range(count) if 0 <= i + step < count]


def flip(block, bit):
    count = lax.axis_size("op")
    return lax.ppermute(block, "op", [(i, i ^ bit) for i in range(count)])


def to_box(block, step):
    return lax.ppermute(block, "box", shifted("box", step))


def prefix(count_ref, upto):
    return lax.fori_loop(0, upto, lambda i, total: total + count_ref[i], 0)


def places(owner_ref, group_ref, box, boxes, capacity):
    before = jnp.maximum(box - 1, 0)
    after = jnp.minimum(box + 1, boxes - 1)
    own_start = prefix(owner_ref, box)
    own_count = owner_ref[box]
    prev_count = jnp.where(box > 0, owner_ref[before], 0)
    prev_start = own_start - jnp.where(box > 0, prev_count, capacity)
    next_start = own_start + own_count
    next_count = jnp.where(box < boxes - 1, owner_ref[after], 0)
    return (
        (prev_start, own_start, next_start),
        (prev_count, own_count, next_count),
        prefix(group_ref, box),
    )


def pinned(*values):
    return tuple(pltpu.with_memory_space_constraint(value, pltpu.HBM) for value in values)


def select_kernel(
    owner_hbm,
    group_hbm,
    target_hbm,
    source_hbm,
    pick_ref,
    side_ref,
    owner_ref,
    group_ref,
    target_ref,
    source_ref,
    sems,
    *,
    boxes,
    capacity,
    quarter,
    span,
):
    pairs = (
        (target_hbm, target_ref),
        (source_hbm, source_ref),
        (owner_hbm, owner_ref),
        (group_hbm, group_ref),
    )
    copies = [
        pltpu.make_async_copy(source, target, sems.at[i]) for i, (source, target) in enumerate(pairs)
    ]
    for copy in copies:
        copy.start()
    for copy in copies:
        copy.wait()
    box = lax.axis_index("box")
    core = lax.axis_index("op") % 2
    starts, _, group_start = places(owner_ref, group_ref, box, boxes, capacity)
    first = group_start - capacity // 3
    found = jnp.where(target_ref[0] < capacity, source_ref[0] - first, -1)
    offsets = found.shape[0]
    found = jnp.concatenate(
        [found, jnp.full((offsets, padded(capacity) - capacity), -1, jnp.int32)], axis=1
    )
    columns = found.T
    row = lax.broadcasted_iota(jnp.int32, (capacity, span), 1)
    for k in range(offsets):
        hit = columns[:capacity, k : k + 1] == row
        pick_ref[k] = jnp.where(hit, 1.0, 0.0).astype(jnp.bfloat16)
    bound = group_start + group_ref[box] - starts[1]
    slot = quarter * core + lax.broadcasted_iota(jnp.int32, side_ref.shape, 0)
    side_ref[...] = jnp.where(slot >= bound, 1.0, 0.0)


def selections(owner_count, group_count, target_slot, source_box, boxes, quarter, span):
    _, offsets, capacity = target_slot.shape
    hbm = pl.BlockSpec(memory_space=pltpu.HBM)
    vmem = pl.BlockSpec(memory_space=pltpu.VMEM)
    return pl.pallas_call(
        functools.partial(
            select_kernel, boxes=boxes, capacity=capacity, quarter=quarter, span=span
        ),
        in_specs=[hbm] * 4,
        out_specs=[vmem] * 2,
        out_shape=[
            jax.ShapeDtypeStruct((offsets, capacity, span), jnp.bfloat16),
            jax.ShapeDtypeStruct((quarter, LANES), jnp.float32),
        ],
        scratch_shapes=[
            pltpu.SMEM(owner_count.shape, jnp.int32),
            pltpu.SMEM(group_count.shape, jnp.int32),
            pltpu.VMEM(target_slot.shape, jnp.int32),
            pltpu.VMEM(source_box.shape, jnp.int32),
            pltpu.SemaphoreType.DMA((4,)),
        ],
        compiler_params=pltpu.CompilerParams(vmem_limit_bytes=GRANT),
        cost_estimate=pl.CostEstimate(
            flops=0, transcendentals=0, bytes_accessed=2 * offsets * capacity * span
        ),
        name="selections",
    )(*pinned(owner_count, group_count, target_slot, source_box))


def split_kernel(op_hbm, main_ref, rest_ref, op_ref, sems, *, whole, room):
    offsets, size, _ = op_ref.shape
    tail = size - whole

    def fetch(k):
        return pltpu.make_async_copy(op_hbm.at[k], op_ref.at[k], sems.at[k])

    for k in range(offsets):
        fetch(k).start()

    def split(k, carry):
        fetch(k).wait()
        block = op_ref[k]
        high = block.astype(jnp.bfloat16)
        wide = high.astype(jnp.float32)
        low = block - wide
        space = jnp.zeros((size, LANES - tail), jnp.float32)
        high_tail = jnp.concatenate([wide[:, whole:], space], axis=1)
        low_tail = jnp.concatenate([low[:, whole:], space], axis=1)
        ends = high_tail + pltpu.roll(high_tail, tail, 1) + pltpu.roll(low_tail, 2 * tail, 1)
        low = low[:, :whole].astype(jnp.bfloat16)
        ends = ends.astype(jnp.bfloat16)
        main_ref[k, :, :whole] = high[:whole, :whole]
        main_ref[k, :, whole : 2 * whole] = low[:whole]
        main_ref[k, :, 2 * whole :] = ends[:whole]
        blank = jnp.zeros((room - tail, whole), jnp.bfloat16)
        rest_ref[k, :room, :whole] = jnp.concatenate([high[whole:, :whole], blank], axis=0)
        rest_ref[k, room:, :whole] = jnp.concatenate([low[whole:], blank], axis=0)
        rest_ref[k, :room, whole:] = jnp.concatenate([ends[whole:], blank[:, :LANES]], axis=0)
        rest_ref[k, room:, whole:] = jnp.zeros((room, LANES), jnp.bfloat16)
        return carry

    lax.fori_loop(0, offsets, split, 0)


def split_operators(operators):
    offsets, size, _ = operators.shape
    whole = size // LANES * LANES
    room = padded(size - whole, 16)
    hbm = pl.BlockSpec(memory_space=pltpu.HBM)
    vmem = pl.BlockSpec(memory_space=pltpu.VMEM)
    return pl.pallas_call(
        functools.partial(split_kernel, whole=whole, room=room),
        in_specs=[hbm],
        out_specs=[vmem] * 2,
        out_shape=[
            jax.ShapeDtypeStruct((offsets, whole, 2 * whole + LANES), jnp.bfloat16),
            jax.ShapeDtypeStruct((offsets, 2 * room, whole + LANES), jnp.bfloat16),
        ],
        scratch_shapes=[
            pltpu.VMEM(operators.shape, jnp.float32),
            pltpu.SemaphoreType.DMA((offsets,)),
        ],
        compiler_params=pltpu.CompilerParams(vmem_limit_bytes=GRANT),
        cost_estimate=pl.CostEstimate(
            flops=0, transcendentals=0, bytes_accessed=4 * offsets * size * size
        ),
        name="split_operators",
    )(*pinned(operators))


def translate_kernel(
    owner_ref,
    group_ref,
    own_ref,
    near_ref,
    weight_ref,
    rest_ref,
    pick_ref,
    send_ref,
    keep_ref,
    window,
    packed,
    total,
    ends,
    *,
    boxes,
    capacity,
    quarter,
    size,
    span,
    need,
    batch,
):
    box = lax.axis_index("box")
    device = lax.axis_index("op")
    core = device % 2
    whole = size // LANES * LANES
    tail = size - whole
    third = capacity // 3
    tiles = padded(size) // LANES
    room = rest_ref.shape[1] // 2
    starts, counts, group_start = places(owner_ref, group_ref, box, boxes, capacity)

    def columns(tile):
        return slice(tile * LANES, min((tile + 1) * LANES, size))

    margin = 2 * third
    for owner in range(3):
        source, blocks = (own_ref, 1) if owner == 1 else (near_ref, 2)
        for part in range(4):
            at = margin + starts[owner] + quarter * part - (group_start - third)
            at = jnp.clip(at, 0, window.shape[1] - quarter)
            mask = device ^ part
            order = 2 * (mask % 2) + mask // 2
            line = pl.multiple_of(quarter * (blocks * order + (1 if owner == 2 else 0)), 8)
            for tile in range(tiles):
                lanes = columns(tile)
                window[tile, pl.ds(at, quarter), : lanes.stop - lanes.start] = source[
                    pl.ds(line, quarter), lanes
                ]

    def pack(index, carry):
        base = pl.multiple_of(index * LANES, LANES)
        inside = pl.ds(base, LANES)
        row = base + lax.broadcasted_iota(jnp.int32, (LANES, LANES), 0)
        lane = lax.broadcasted_iota(jnp.int32, (LANES, LANES), 1)
        for tile in range(tiles):
            fine = row < need
            if tile == tiles - 1:
                fine = fine & (lane < tail)
            value = jnp.where(fine, window[tile, pl.ds(margin + base, LANES), :], 0.0)
            high = value.astype(jnp.bfloat16)
            low = value - high.astype(jnp.float32)
            if tile < tiles - 1:
                packed[inside, tile * LANES : (tile + 1) * LANES] = high
                packed[inside, whole + tile * LANES : whole + (tile + 1) * LANES] = low.astype(
                    jnp.bfloat16
                )
            else:
                high = high.astype(jnp.float32)
                rest = high + pltpu.roll(low, tail, 1) + pltpu.roll(high, 2 * tail, 1)
                packed[inside, 2 * whole :] = rest.astype(jnp.bfloat16)
        return carry

    lax.fori_loop(0, span // LANES, pack, 0)
    total[:, capacity : 2 * capacity, :] = jnp.zeros((tiles, capacity, LANES), jnp.float32)
    ends[...] = jnp.zeros(ends.shape, jnp.float32)

    def product(left, right):
        return lax.dot_general(
            jnp.concatenate(left, axis=1),
            jnp.concatenate(right, axis=1),
            (((1,), (1,)), ((), ())),
            preferred_element_type=jnp.float32,
        )

    def offsets(index, carry):
        base = index * batch
        several = range(batch)
        picks = pick_ref[pl.ds(base, batch)].reshape(batch * capacity, span)
        picked = jnp.dot(picks, packed[...], preferred_element_type=jnp.float32).astype(jnp.bfloat16)
        rows = [picked[i * capacity : (i + 1) * capacity] for i in several]
        high = [value[:, :whole] for value in rows]
        last = [value[:, 2 * whole :] for value in rows]
        both = [jnp.concatenate([value[:, :whole], value[:, whole : 2 * whole]], axis=0) for value in rows]
        wide = product(both, [weight_ref[base + i, :, :whole] for i in several])
        part = wide[:capacity] + wide[capacity:]
        part += product(
            high + last,
            [weight_ref[base + i, :, whole : 2 * whole] for i in several]
            + [weight_ref[base + i, :, 2 * whole :] for i in several],
        )
        for tile in range(tiles - 1):
            total[tile, capacity : 2 * capacity, :] += part[:, tile * LANES : (tile + 1) * LANES]
        wide = product(both, [rest_ref[base + i, :, :whole] for i in several])
        ends[:, : 2 * room] += (
            wide[:capacity]
            + wide[capacity:]
            + product(last, [rest_ref[base + i, :, whole:] for i in several])
        )
        return carry

    lax.fori_loop(0, pick_ref.shape[0] // batch, offsets, 0)
    both = ends[...]
    total[tiles - 1, capacity : 2 * capacity, :] = both + pltpu.roll(both, LANES - room, 1)

    slot = lax.broadcasted_iota(jnp.int32, (quarter, LANES), 0)

    def place(ref, first, parts):
        spots = []
        for owner, block in parts:
            shift = starts[owner] - group_start + quarter * block
            low = jnp.maximum(-shift, 0)
            high = jnp.minimum(counts[owner] - quarter * block, capacity - shift)
            at = jnp.clip(capacity + shift, 0, total.shape[1] - quarter)
            spots.append((at, (slot >= low) & (slot < high)))
        for tile in range(tiles):
            lanes = columns(tile)
            value = sum(
                jnp.where(fine, total[tile, pl.ds(at, quarter), :], 0.0) for at, fine in spots
            )
            ref[first : first + quarter, lanes] = value[:, : lanes.stop - lanes.start]

    for ref, side in ((send_ref, 1 - core), (keep_ref, core)):
        place(ref, 0, [(1, side)])
        place(ref, quarter, [(1, side + 2)])
        place(ref, 2 * quarter, [(0, side), (0, side + 2)])
        place(ref, 3 * quarter, [(2, side)])


def translate(owner_count, group_count, own, near, weights, rests, picks, boxes):
    offsets, capacity, span = picks.shape
    size = own.shape[1]
    quarter = own.shape[0] // 4
    need = capacity + 2 * (capacity // 3)
    tiles = padded(size) // LANES
    smem = pl.BlockSpec(memory_space=pltpu.SMEM)
    vmem = pl.BlockSpec(memory_space=pltpu.VMEM)
    return pl.pallas_call(
        functools.partial(
            translate_kernel,
            boxes=boxes,
            capacity=capacity,
            quarter=quarter,
            size=size,
            span=span,
            need=need,
            batch=math.gcd(offsets, BATCH),
        ),
        in_specs=[smem, smem] + [vmem] * 5,
        out_specs=[vmem, vmem],
        out_shape=[jax.ShapeDtypeStruct((capacity, size), jnp.float32)] * 2,
        scratch_shapes=[
            pltpu.VMEM((tiles, 3 * capacity, LANES), jnp.float32),
            pltpu.VMEM((span, weights.shape[2]), jnp.bfloat16),
            pltpu.VMEM((tiles, 3 * capacity, LANES), jnp.float32),
            pltpu.VMEM((capacity, LANES), jnp.float32),
        ],
        compiler_params=pltpu.CompilerParams(vmem_limit_bytes=GRANT),
        name="translate",
    )(owner_count, group_count, own, near, weights, rests, picks)


def body(density, operators, owner_count, group_count, target_slot, source_box):
    quarter = density.shape[0]
    parts = lax.axis_size("op")
    boxes = lax.axis_size("box")
    capacity = quarter * parts
    if parts != 4:
        raise ValueError("unsupported op axis")
    span = padded(capacity + 2 * (capacity // 3))
    device = lax.axis_index("op")

    earlier = to_box(density, 1)
    later = to_box(density, -1)
    across = flip(density, 2)
    near = jnp.concatenate([earlier, later], axis=0)
    own = jnp.concatenate([density, across], axis=0)
    picks, side = selections(
        owner_count, group_count, target_slot, source_box, boxes, quarter, span
    )
    near, own, picks = lax.optimization_barrier((near, own, picks))
    near_across = flip(near, 2)
    own_peer = flip(own, 1)
    weights, rests = split_operators(operators)
    near_across, own_peer, weights, rests = lax.optimization_barrier(
        (near_across, own_peer, weights, rests)
    )
    own = jnp.concatenate([own, own_peer], axis=0)
    near = jnp.concatenate([near, near_across], axis=0)
    near = jnp.concatenate([near, flip(near, 1)], axis=0)
    send, keep = translate(owner_count, group_count, own, near, weights, rests, picks, boxes)
    both = keep + flip(send, 1)
    low, high, down, up = (both[i * quarter : (i + 1) * quarter] for i in range(4))
    from_after = to_box(down, -1)
    from_before = to_box(up, 1)
    early = side[:, :1] > 0.5
    low = low + from_before + jnp.where(early, from_after, 0.0)
    high = high + jnp.where(early, 0.0, from_after)
    first = device < 2
    return jnp.where(first, low, high) + flip(jnp.where(first, high, low), 2)


def solution(mesh):
    placed = (
        P(("box", "op"), None),
        P("op", None, None),
        P(),
        P(),
        P("box", "op", None),
        P("box", "op", None),
    )
    return jax.shard_map(
        body, mesh=mesh, in_specs=placed, out_specs=P(("box", "op"), None), check_vma=False
    )
```
